256 devices in a mesh: ctx: 32 (over y, x, core), tp: 8 (over z).
Axes of the slice: x: 4, y: 4, z: 8, core: 2. Of those that a mesh axis runs over, the one named last changes fastest.
Arguments:
- queries: bfloat16 [1, 32768, 4096], P(None, 'ctx', 'tp'), may hold values from -6 to 6
- keys: bfloat16 [1, 32768, 1024], P(None, 'ctx', 'tp'), may hold values from -6 to 6
- values: bfloat16 [1, 32768, 1024], P(None, 'ctx', 'tp'), may hold values from -6 to 6
- gates: int32 [1, 64, 8, 3], P(None, 'ctx', 'tp'), may hold values from 0 to 63, as said below
- out_weight: bfloat16 [4096, 4096], P('tp'), may hold values from -0.09375 to 0.09375
Outputs:
- projected: bfloat16 [1, 32768, 4096], P(None, 'ctx', 'tp')
The draws below stay inside these ranges and needn't reach their ends.
Inputs may be any that keep to these rules, and one draw needn't show every extreme that they name: `gates`: for each sequence and key-value head, the 6 entries of query blocks 2 c to 2 c + 1 name blocks of 6 different values of (block // 2).
All inputs are finite; a program needn't handle non-finite values.
Results may differ from the reference program's by a relative error of at most 0.015.
Values may be sent and summed in bfloat16 or wider, within the bound.
No kernel may reach another device: no remote copies, remote signals or barrier semaphores. Data moves between devices by JAX's collectives and lax.ppermute only.
A program may use at most 64 MiB of HBM per device.

```python
import jax
import jax.numpy as jnp
from jax import lax

HQ = 32
KVH = 8
HD = 128
D_OUT = 4096
TOKB = 512
PICKS = 3
QB_DEV = 2
SEQ = 1
NB = 64
L = 32768
N_TP = 8


def draw_queries(key, part):
    drawn = jax.random.truncated_normal(jax.random.fold_in(key, 11), -6.0, 6.0, (SEQ, L, HQ * HD), jnp.float32)
    return drawn.astype(jnp.bfloat16)


def draw_keys(key, part):
    drawn = jax.random.truncated_normal(jax.random.fold_in(key, 13), -6.0, 6.0, (SEQ, L, KVH * HD), jnp.float32)
    return drawn.astype(jnp.bfloat16)


def draw_gates(key, part):
    device_count = NB // QB_DEV
    pick_total = PICKS * QB_DEV
    random_scores = jax.random.randint(jax.random.fold_in(key, 21), (SEQ, device_count, KVH, device_count), 0, 2 ** 17)
    column = jnp.arange(device_count, dtype=jnp.int32)
    row_of = column[None, :, None, None]
    col_of = column[None, None, None, :]
    ranked = random_scores * 4096 + col_of
    forced = (row_of == 0) & (col_of == device_count - 1) | (row_of == device_count - 1) & (col_of == 0)
    ranked = jnp.where(forced, ranked + 2 ** 30, ranked)
    reachable = jnp.where(column == 0, device_count, jnp.maximum(column, pick_total))
    allowed = col_of < reachable[None, :, None, None]
    ranked = jnp.where(allowed, ranked, -1 - col_of)
    chosen = lax.top_k(ranked, pick_total)[1].astype(jnp.int32)
    offsets = jax.random.randint(jax.random.fold_in(key, 23), chosen.shape, 0, QB_DEV)
    row_pick = jnp.broadcast_to(column[None, :, None, None], chosen.shape)
    offsets = jnp.where((row_pick == 0) & (chosen == device_count - 1), QB_DEV - 1, offsets)
    offsets = jnp.where((row_pick == device_count - 1) & (chosen == 0), 0, offsets)
    picked = (chosen * QB_DEV + offsets).astype(jnp.int32)
    picked = picked.reshape(SEQ, device_count, KVH, QB_DEV, PICKS)
    return jnp.transpose(picked, (0, 1, 3, 2, 4)).reshape(SEQ, NB, KVH, PICKS)


def block_scale(stream_key, extent, shards, smallest, high):
    def one(dim, blocks):
        heights = jax.random.uniform(jax.random.fold_in(jax.random.fold_in(stream_key, 6), dim), (blocks,), jnp.float32, smallest / len(shards), high / len(shards))
        return jnp.repeat(jnp.exp(heights), extent[dim] // blocks).reshape((-1,) + (1,) * (len(extent) - dim - 1))

    loudness = one(*shards[0])
    for cut in shards[1:]:
        loudness = loudness * one(*cut)
    return loudness


def centred(stream_key, extent, width, most, split=(), held_as=jnp.bfloat16):
    result = jax.random.normal(stream_key, extent, jnp.float32) * width
    if len(split) > 0:
        result = block_scale(stream_key, extent, split, -0.22, 0.18) * result
    return jnp.clip(result, min=-most, max=most).astype(held_as)


def setup_inputs(seed: int = 0) -> dict:
    key_list = jax.random.split(jax.random.key(seed), 6)
    queries = draw_queries(jax.random.fold_in(key_list[5], 71), 0)
    keys = draw_keys(jax.random.fold_in(key_list[5], 71), 0)
    values = centred(key_list[2], (SEQ, L, KVH * HD), 1.0, 6.0, ((1, 32), (2, 8)))
    gates = draw_gates(jax.random.fold_in(key_list[5], 71), 0)
    out_weight = centred(key_list[4], (HQ * HD, D_OUT), (HQ * HD) ** -0.5, 0.09375, ((0, 8),))
    return {"queries": queries, "keys": keys, "values": values, "gates": gates, "out_weight": out_weight}


def attend_rows(query_block, key_rows, value_rows, allowed):
    score_scale = HD ** -0.5
    scores = jnp.einsum("qhgd,hkd->hgqk", query_block.astype(jnp.float32), key_rows.astype(jnp.float32)) * score_scale
    scores = jnp.where(allowed[:, None], scores, -jnp.inf)
    largest = jnp.max(scores, axis=-1, keepdims=True)
    raw_weights = jnp.exp(scores - largest)
    denominator = jnp.sum(raw_weights, axis=-1)
    weights = raw_weights.astype(jnp.bfloat16)
    weighted = jnp.einsum("hgqk,hkd->qhgd", weights.astype(jnp.float32), value_rows.astype(jnp.float32))
    weighted = weighted / jnp.transpose(denominator, (2, 0, 1))[..., None]
    return weighted.astype(jnp.bfloat16).reshape(TOKB, -1)


def reference(queries, keys, values, gates, out_weight):
    head_group = HQ // KVH
    causal = jnp.arange(TOKB)[:, None] >= jnp.arange(TOKB)[None, :]
    head_index = jnp.arange(KVH, dtype=jnp.int32)

    def one_sequence(inputs):
        seq_queries, seq_keys, seq_values, seq_gates = inputs
        key_blocks = seq_keys.reshape(NB, TOKB, KVH, HD)
        value_blocks = seq_values.reshape(NB, TOKB, KVH, HD)
        query_blocks = seq_queries.reshape(NB, TOKB, KVH, head_group, HD)

        def one_block(block_index):
            selected = seq_gates[block_index]
            own_keys = jnp.transpose(key_blocks[block_index], (1, 0, 2))
            own_values = jnp.transpose(value_blocks[block_index], (1, 0, 2))
            picked_keys = key_blocks[selected, :, head_index[:, None], :]
            picked_values = value_blocks[selected, :, head_index[:, None], :]
            key_rows = jnp.concatenate([own_keys[:, None], picked_keys], axis=1).reshape(KVH, (1 + PICKS) * TOKB, HD)
            value_rows = jnp.concatenate([own_values[:, None], picked_values], axis=1).reshape(KVH, (1 + PICKS) * TOKB, HD)
            usable = selected < block_index
            pick_allow = jnp.broadcast_to(usable[:, None, :, None], (KVH, TOKB, PICKS, TOKB)).reshape(KVH, TOKB, PICKS * TOKB)
            own_allow = jnp.broadcast_to(causal[None], (KVH, TOKB, TOKB))
            allowed = jnp.concatenate([own_allow, pick_allow], axis=2)
            return attend_rows(query_blocks[block_index], key_rows, value_rows, allowed)

        blocks_out = lax.map(one_block, jnp.arange(NB, dtype=jnp.int32))
        return blocks_out.reshape(L, HQ * HD)

    attended = lax.map(one_sequence, (queries, keys, values, gates))
    share = HQ * HD // N_TP
    features = jnp.transpose(attended.reshape(SEQ * L, N_TP, share), (1, 0, 2))
    weight_parts = out_weight.reshape(N_TP, share, D_OUT)

    def accumulate(summed, inputs):
        feature_part, weight_part = inputs
        partial_value = jnp.dot(feature_part, weight_part, preferred_element_type=jnp.float32).astype(jnp.bfloat16)
        partial_value = lax.optimization_barrier(partial_value)
        return summed + partial_value.astype(jnp.float32), None

    summed, _ = lax.scan(accumulate, jnp.zeros((SEQ * L, D_OUT), jnp.float32), (features, weight_parts))
    return summed.astype(jnp.bfloat16).reshape(SEQ, L, D_OUT)
```

```python
import jax
import jax.numpy as jnp
from jax import lax
from jax.experimental import pallas as pl
from jax.experimental.pallas import tpu as pltpu
from jax.sharding import PartitionSpec as P

HD = 128
TOKB = 512
PICKS = 3
NX, NY, NC = 4, 4, 2
HEADS = 4
SUB = 256
LOG2E = 1.4426950408889634
FAR = 1e30


def ctx_perm(dy, dx, dc):
    pairs = []
    for y in range(NY):
        for x in range(NX):
            for c in range(NC):
                src = (y * NX + x) * NC + c
                dst = (((y + dy) % NY) * NX + (x + dx) % NX) * NC + (c + dc) % NC
                pairs.append((src, dst))
    return pairs


def shift(v, dy, dx, dc=0):
    return lax.ppermute(v, "ctx", ctx_perm(dy, dx, dc))


def torus_gather(own, first, second):
    def go(v, axis, s):
        return shift(v, s, 0) if axis == "y" else shift(v, 0, s)

    fwd = go(own, first, 1)
    bwd = go(own, first, -1)
    far0 = go(fwd[:1], first, 1)
    far1 = go(bwd[1:], first, -1)
    near = jnp.stack([own, fwd])
    rest = jnp.stack([bwd, jnp.concatenate([far0, far1])])
    up_near = go(near, second, 1)
    dn_near = go(near, second, -1)
    dn_rest = go(rest, second, -1)
    up_rest = go(rest, second, 1)
    far_near = go(up_near, second, 1)
    far_rest = go(dn_rest, second, -1)
    return [near, rest, up_near, up_rest, dn_near, dn_rest, far_near, far_rest]


def place_code(delta):
    return jnp.where(delta == 3, 2, jnp.where(delta == 2, 3, delta))


def pick_codes(blocks, y, x):
    sy = blocks // 16
    sx = (blocks // 4) % 4
    core = (blocks // 2) % 2
    half = blocks % 2
    cy = place_code((y - sy) % 4)
    cx = place_code((x - sx) % 4)
    k_arr = cy * 2 + cx // 2
    k_slot = (cx % 2) * 2 + half
    v_arr = cx * 2 + cy // 2
    v_slot = (cy % 2) * 2 + half
    return k_arr, k_slot, v_arr, v_slot, core


def start_from(arrays, arr, slot, dst, sem):
    for n, ref in enumerate(arrays):

        @pl.when(arr == n)
        def _(ref=ref):
            pltpu.make_async_copy(ref.at[slot], dst, sem).start()


def gather_body(codes, *refs):
    k_arrays, v_arrays, out, sems = refs[:8], refs[8:16], refs[16], refs[17]
    count = 2 * PICKS
    for j in range(count):

        @pl.when(codes[4, j] != 0)
        def _(j=j):
            start_from(k_arrays, codes[0, j], codes[1, j], out.at[j, 0], sems.at[j, 0])
            start_from(v_arrays, codes[2, j], codes[3, j], out.at[j, 1], sems.at[j, 1])

    for j in range(count):

        @pl.when(codes[4, j] != 0)
        def _(j=j):
            for t in range(2):
                pltpu.make_async_copy(k_arrays[0].at[0], out.at[j, t], sems.at[j, t]).wait()


def gather_picks(codes, k_arrays, v_arrays):
    any_spec = pl.BlockSpec(memory_space=pl.ANY)
    return pl.pallas_call(
        gather_body,
        out_shape=jax.ShapeDtypeStruct((2 * PICKS, 2, TOKB, HD), jnp.bfloat16),
        grid_spec=pltpu.PrefetchScalarGridSpec(
            num_scalar_prefetch=1,
            grid=(1,),
            in_specs=[any_spec] * 16,
            out_specs=any_spec,
            scratch_shapes=[pltpu.SemaphoreType.DMA((2 * PICKS, 2))],
        ),
        name="gather_picks",
    )(codes, *k_arrays, *v_arrays)


def attend_body(codes, q, k_own, v_own, *refs):
    k_arrays, v_arrays, partner = refs[:8], refs[8:16], refs[16]
    out, k_buf, v_buf, sems = refs[17], refs[18], refs[19], refs[20]

    @pl.when(pl.program_id(0) == 0)
    def _():
        for j in range(PICKS):
            rows = pl.ds((j + 1) * TOKB, TOKB)
            k_dst = k_buf.at[rows, :]
            v_dst = v_buf.at[rows, pl.ds(0, HD)]

            @pl.when(codes[4, j] != 0)
            def _(j=j, k_dst=k_dst, v_dst=v_dst):
                start_from(k_arrays, codes[0, j], codes[1, j], k_dst, sems.at[j, 0])
                start_from(v_arrays, codes[2, j], codes[3, j], v_dst, sems.at[j, 1])

            @pl.when(codes[4, j] == 0)
            def _(j=j, k_dst=k_dst, v_dst=v_dst):
                slot = codes[6, j]
                pltpu.make_async_copy(partner.at[slot, 0], k_dst, sems.at[j, 0]).start()
                pltpu.make_async_copy(partner.at[slot, 1], v_dst, sems.at[j, 1]).start()

        k_buf[:TOKB, :] = k_own[...]
        v_buf[:TOKB, :HD] = v_own[...]
        v_buf[:, HD:] = jnp.ones((v_buf.shape[0], HD), jnp.bfloat16)
        for j in range(PICKS):
            rows = pl.ds((j + 1) * TOKB, TOKB)
            pltpu.make_async_copy(partner.at[0, 0], k_buf.at[rows, :], sems.at[j, 0]).wait()
            v_dst = v_buf.at[rows, pl.ds(0, HD)]
            pltpu.make_async_copy(partner.at[0, 0], v_dst, sems.at[j, 1]).wait()

    c = HD**-0.5 * LOG2E
    contract = (((1,), (1,)), ((), ()))
    for part in range(TOKB // SUB):
        rows = slice(part * SUB, (part + 1) * SUB)
        own_len = (part + 1) * SUB
        q_tile = q[rows, :]
        pieces = []
        s_own = lax.dot_general(
            q_tile, k_buf[:own_len, :], contract, preferred_element_type=jnp.float32
        )
        row = lax.broadcasted_iota(jnp.int32, (SUB, own_len), 0) + part * SUB
        col = lax.broadcasted_iota(jnp.int32, (SUB, own_len), 1)
        s_own = jnp.where(row >= col, s_own, -FAR)
        largest = jnp.max(s_own, axis=1, keepdims=True)
        for j in range(PICKS):
            s_pick = lax.dot_general(
                q_tile,
                k_buf[(j + 1) * TOKB : (j + 2) * TOKB, :],
                contract,
                preferred_element_type=jnp.float32,
            )
            usable = codes[5, j] != 0
            peak = jnp.max(s_pick, axis=1, keepdims=True)
            largest = jnp.maximum(largest, jnp.where(usable, peak, -FAR))
            pieces.append((s_pick, usable))
        base = largest * c
        w_own = jnp.exp2(s_own * c - base).astype(jnp.bfloat16)
        total = jnp.dot(w_own, v_buf[:own_len, :], preferred_element_type=jnp.float32)
        for j, (s_pick, usable) in enumerate(pieces):
            shift_by = jnp.where(usable, base, FAR)
            w = jnp.exp2(s_pick * c - shift_by).astype(jnp.bfloat16)
            total += jnp.dot(
                w,
                v_buf[(j + 1) * TOKB : (j + 2) * TOKB, :],
                preferred_element_type=jnp.float32,
            )
        out[rows, :] = (total[:, :HD] / total[:, HD:]).astype(jnp.bfloat16)


def attend(chunk, codes, q, k, v, k_arrays, v_arrays, partner):
    any_spec = pl.BlockSpec(memory_space=pl.ANY)
    keys_all = (1 + PICKS) * TOKB
    return pl.pallas_call(
        attend_body,
        out_shape=jax.ShapeDtypeStruct((TOKB, HEADS * HD), jnp.bfloat16),
        grid_spec=pltpu.PrefetchScalarGridSpec(
            num_scalar_prefetch=1,
            grid=(HEADS,),
            in_specs=[
                pl.BlockSpec((TOKB, HD), lambda h, s: (chunk, h)),
                pl.BlockSpec((TOKB, HD), lambda h, s: (chunk, 0)),
                pl.BlockSpec((TOKB, HD), lambda h, s: (chunk, 0)),
            ]
            + [any_spec] * 17,
            out_specs=pl.BlockSpec((TOKB, HD), lambda h, s: (0, h)),
            scratch_shapes=[
                pltpu.VMEM((keys_all, HD), jnp.bfloat16),
                pltpu.VMEM((keys_all, 2 * HD), jnp.bfloat16),
                pltpu.SemaphoreType.DMA((PICKS, 2)),
            ],
        ),
        name="attend",
    )(codes, q, k, v, *k_arrays, *v_arrays, partner)


def per_device(queries, keys, values, gates, out_weight):
    q = queries[0]
    k = keys[0]
    v = values[0]
    tp_count = lax.axis_size("tp")
    ctx = lax.axis_index("ctx")
    me = lax.axis_index("tp")
    y, x, core = ctx // 8, (ctx // 2) % 4, ctx % 2
    picked = gates.reshape(2 * PICKS)
    partner_picked = shift(picked, 0, 0, 1)

    k_arrays = torus_gather(k.reshape(2, TOKB, HD), "x", "y")
    v_arrays = torus_gather(v.reshape(2, TOKB, HD), "y", "x")
    k_arrays = [a.reshape(4, TOKB, HD) for a in k_arrays]
    v_arrays = [a.reshape(4, TOKB, HD) for a in v_arrays]

    def table(blocks):
        ka, ks, va, vs, source_core = pick_codes(blocks, y, x)
        here = (source_core == core).astype(jnp.int32)
        query_block = ctx * 2 + jnp.arange(2 * PICKS, dtype=jnp.int32) // PICKS
        usable = (blocks < query_block).astype(jnp.int32)
        slot = jnp.arange(2 * PICKS, dtype=jnp.int32)
        return jnp.stack([ka, ks, va, vs, here, usable, slot]).astype(jnp.int32)

    own_codes = table(picked)
    to_partner = gather_picks(table(partner_picked), k_arrays, v_arrays)
    from_partner = shift(to_partner, 0, 0, 1)

    share = out_weight.shape[1] // tp_count
    ring_up = [(i, (i + 1) % tp_count) for i in range(tp_count)]
    ring_dn = [(i, (i - 1) % tp_count) for i in range(tp_count)]
    outs = []
    for chunk in range(2):
        chunk_codes = own_codes[:, chunk * PICKS : (chunk + 1) * PICKS]
        attended = attend(chunk, chunk_codes, q, k, v, k_arrays, v_arrays, from_partner)

        def part(offset, attended=attended):
            w = lax.dynamic_slice_in_dim(out_weight, ((me + offset) % tp_count) * share, share, 1)
            return jnp.dot(attended, w, preferred_element_type=jnp.float32)

        far = part(4).astype(jnp.bfloat16)
        half = share // 2
        up = lax.ppermute(far[:, :half], "tp", ring_up)
        dn = lax.ppermute(far[:, half:], "tp", ring_dn)
        zeros = jnp.zeros((TOKB, half), jnp.bfloat16)
        up = jnp.concatenate([up, zeros], axis=1)
        dn = jnp.concatenate([zeros, dn], axis=1)
        for d in (3, 2, 1):
            up = lax.ppermute(
                (part(d) + up.astype(jnp.float32)).astype(jnp.bfloat16), "tp", ring_up
            )
            dn = lax.ppermute(
                (part(-d) + dn.astype(jnp.float32)).astype(jnp.bfloat16), "tp", ring_dn
            )
        outs.append((part(0) + up.astype(jnp.float32) + dn.astype(jnp.float32)).astype(jnp.bfloat16))
    return jnp.concatenate(outs, axis=0)[None]


def solution(mesh):
    placed = (
        P(None, "ctx", "tp"),
        P(None, "ctx", "tp"),
        P(None, "ctx", "tp"),
        P(None, "ctx", "tp", None),
        P("tp", None),
    )
    return jax.shard_map(
        per_device, mesh=mesh, in_specs=placed, out_specs=P(None, "ctx", "tp"), check_vma=False
    )
```

```python
import jax
import jax.numpy as jnp
from jax import lax
from jax.experimental import pallas as pl
from jax.experimental.pallas import tpu as pltpu
from jax.sharding import PartitionSpec as P

HD = 128
TOKB = 512
PICKS = 3
NX, NY, NC = 4, 4, 2
HEADS = 4
SUB = 256
LOG2E = 1.4426950408889634
FAR = 1e30


def ctx_perm(move):
    pairs = []
    for y in range(NY):
        for x in range(NX):
            for c in range(NC):
                to_y, to_x, to_c = move(y, x, c)
                dst = ((to_y % NY) * NX + to_x % NX) * NC + to_c % NC
                pairs.append(((y * NX + x) * NC + c, dst))
    return pairs


def swap_cores(v):
    return lax.ppermute(v, "ctx", ctx_perm(lambda y, x, c: (y, x, c + 1)))


def shift_first(v, s):
    move = lambda y, x, c: (y, x + s, c) if c == 0 else (y + s, x, c)
    return lax.ppermute(v, "ctx", ctx_perm(move))


def shift_second(v, s):
    move = lambda y, x, c: (y + s, x, c) if c == 0 else (y, x + s, c)
    return lax.ppermute(v, "ctx", ctx_perm(move))


def torus_gather(own):
    fwd = shift_first(own, 1)
    bwd = shift_first(own, -1)
    near = jnp.concatenate([own, fwd])
    up_near = shift_second(near, 1)
    dn_near = shift_second(near, -1)
    far0 = shift_first(fwd[:2], 1)
    far1 = shift_first(bwd[2:], -1)
    rest = jnp.concatenate([bwd, far0, far1])
    dn_rest = shift_second(rest, -1)
    up_rest = shift_second(rest, 1)
    far_near = shift_second(up_near, 1)
    far_rest = shift_second(dn_rest, -1)
    return [near, rest, up_near, up_rest, dn_near, dn_rest, far_near, far_rest]


def place_code(delta):
    return jnp.where(delta == 3, 2, jnp.where(delta == 2, 3, delta))


def table(blocks, y, x, core, ctx):
    cy = place_code((y - blocks // 16) % 4)
    cx = place_code((x - (blocks // 4) % 4) % 4)
    first = jnp.where(core == 0, cx, cy)
    second = jnp.where(core == 0, cy, cx)
    arr = second * 2 + first // 2
    slot = (first % 2) * 4 + blocks % 4
    number = jnp.arange(2 * PICKS, dtype=jnp.int32)
    usable = (blocks < ctx * 2 + number // PICKS).astype(jnp.int32)
    return jnp.stack([arr, slot, usable, number, jnp.full_like(number, core)]).astype(jnp.int32)


def start_from(arrays, arr, slot, dst, sem):
    for n, ref in enumerate(arrays):

        @pl.when(arr == n)
        def _(ref=ref):
            pltpu.make_async_copy(ref.at[slot], dst, sem).start()


def gather_body(codes, *refs):
    arrays, out, sems = refs[:8], refs[8], refs[9]
    for j in range(2 * PICKS):
        start_from(arrays, codes[0, j], codes[1, j], out.at[j], sems.at[j])
    for j in range(2 * PICKS):
        pltpu.make_async_copy(arrays[0].at[0], out.at[j], sems.at[j]).wait()


def gather_picks(codes, arrays):
    any_spec = pl.BlockSpec(memory_space=pl.ANY)
    return pl.pallas_call(
        gather_body,
        out_shape=jax.ShapeDtypeStruct((2 * PICKS, TOKB, HD), jnp.bfloat16),
        grid_spec=pltpu.PrefetchScalarGridSpec(
            num_scalar_prefetch=1,
            grid=(1,),
            in_specs=[any_spec] * 8,
            out_specs=pl.BlockSpec((2 * PICKS, TOKB, HD), lambda i, s: (0, 0, 0)),
            scratch_shapes=[pltpu.SemaphoreType.DMA((2 * PICKS,))],
        ),
        name="gather_picks",
    )(codes, *arrays)


def attend_body(first_rows, codes, q, k_own, v_own, *refs):
    arrays, partner = refs[:8], refs[8]
    out, k_buf, v_buf, sems = refs[9], refs[10], refs[11], refs[12]

    @pl.when(pl.program_id(0) == 0)
    def _():
        for j in range(PICKS):
            rows = pl.ds((j + 1) * TOKB, TOKB)
            k_dst = k_buf.at[rows, :]
            v_dst = v_buf.at[rows, pl.ds(0, HD)]

            @pl.when(codes[4, j] == 0)
            def _(j=j, k_dst=k_dst, v_dst=v_dst):
                pltpu.make_async_copy(partner.at[codes[3, j]], v_dst, sems.at[j, 1]).start()
                start_from(arrays, codes[0, j], codes[1, j], k_dst, sems.at[j, 0])

            @pl.when(codes[4, j] != 0)
            def _(j=j, k_dst=k_dst, v_dst=v_dst):
                pltpu.make_async_copy(partner.at[codes[3, j]], k_dst, sems.at[j, 0]).start()
                start_from(arrays, codes[0, j], codes[1, j], v_dst, sems.at[j, 1])

        k_buf[:TOKB, :] = k_own[...]
        v_buf[:TOKB, :HD] = v_own[...]
        v_buf[:, HD:] = jnp.ones((v_buf.shape[0], HD), jnp.bfloat16)
        for j in range(PICKS):
            rows = pl.ds((j + 1) * TOKB, TOKB)
            v_dst = v_buf.at[rows, pl.ds(0, HD)]
            pltpu.make_async_copy(partner.at[0], k_buf.at[rows, :], sems.at[j, 0]).wait()
            pltpu.make_async_copy(partner.at[0], v_dst, sems.at[j, 1]).wait()

    c = HD**-0.5 * LOG2E
    contract = (((1,), (1,)), ((), ()))
    for part in range(q.shape[0] // SUB):
        rows = slice(part * SUB, (part + 1) * SUB)
        start = first_rows + part * SUB
        own_len = start + SUB
        q_tile = q[rows, :]
        s = lax.dot_general(
            q_tile, k_buf[:own_len, :], contract, preferred_element_type=jnp.float32
        )
        row = lax.broadcasted_iota(jnp.int32, (SUB, own_len), 0) + start
        col = lax.broadcasted_iota(jnp.int32, (SUB, own_len), 1)
        s = jnp.where(row >= col, s, -FAR)
        largest = jnp.max(s, axis=1, keepdims=True) * c
        w = jnp.exp2(s * c - largest).astype(jnp.bfloat16)
        total = jnp.dot(w, v_buf[:own_len, :], preferred_element_type=jnp.float32)
        for j in range(PICKS):
            keys = slice((j + 1) * TOKB, (j + 2) * TOKB)
            s = lax.dot_general(
                q_tile, k_buf[keys, :], contract, preferred_element_type=jnp.float32
            )
            usable = codes[2, j] != 0
            peak = jnp.max(s, axis=1, keepdims=True) * c
            grown = jnp.maximum(largest, jnp.where(usable, peak, -FAR))
            w = jnp.exp2(s * c - jnp.where(usable, grown, FAR)).astype(jnp.bfloat16)
            added = jnp.dot(w, v_buf[keys, :], preferred_element_type=jnp.float32)
            total = total * jnp.exp2(largest - grown) + added
            largest = grown
        out[rows, :] = (total[:, :HD] / total[:, HD:]).astype(jnp.bfloat16)


def attend(first_row, rows, codes, q, k, v, arrays, partner):
    any_spec = pl.BlockSpec(memory_space=pl.ANY)
    keys_all = (1 + PICKS) * TOKB
    chunk = first_row // TOKB

    def body(*refs):
        attend_body(first_row % TOKB, *refs)

    return pl.pallas_call(
        body,
        out_shape=jax.ShapeDtypeStruct((rows, HEADS * HD), jnp.bfloat16),
        grid_spec=pltpu.PrefetchScalarGridSpec(
            num_scalar_prefetch=1,
            grid=(HEADS,),
            in_specs=[
                pl.BlockSpec((rows, HD), lambda h, s: (first_row // rows, h)),
                pl.BlockSpec((TOKB, HD), lambda h, s: (chunk, 0)),
                pl.BlockSpec((TOKB, HD), lambda h, s: (chunk, 0)),
            ]
            + [any_spec] * 9,
            out_specs=pl.BlockSpec((rows, HD), lambda h, s: (0, h)),
            scratch_shapes=[
                pltpu.VMEM((keys_all, HD), jnp.bfloat16),
                pltpu.VMEM((keys_all, 2 * HD), jnp.bfloat16),
                pltpu.SemaphoreType.DMA((PICKS, 2)),
            ],
        ),
    )(codes[:, chunk * PICKS : (chunk + 1) * PICKS], q, k, v, *arrays, partner)


RINGS = ((0, 256), (256, 256), (512, 512))


def layer(queries, keys, values, gates, out_weight):
    q = queries[0]
    k = keys[0]
    v = values[0]
    tp_count = lax.axis_size("tp")
    ctx = lax.axis_index("ctx")
    me = lax.axis_index("tp")
    y, x, core = ctx // 8, (ctx // 2) % 4, ctx % 2
    picked = gates.reshape(2 * PICKS)

    kept = jnp.where(core == 0, k, v).reshape(2, TOKB, HD)
    given = jnp.where(core == 0, v, k).reshape(2, TOKB, HD)
    got = swap_cores(given)
    own = jnp.concatenate([jnp.where(core == 0, kept, got), jnp.where(core == 0, got, kept)])
    partner_picked = swap_cores(picked)
    arrays = torus_gather(own)

    own_codes = table(picked, y, x, core, ctx)
    to_partner = gather_picks(table(partner_picked, y, x, core, ctx), arrays)
    from_partner = swap_cores(to_partner)

    share = out_weight.shape[1] // tp_count
    half = share // 2
    ring_up = [(i, (i + 1) % tp_count) for i in range(tp_count)]
    ring_dn = [(i, (i - 1) % tp_count) for i in range(tp_count)]
    weights = {
        d: lax.dynamic_slice_in_dim(out_weight, ((me + d) % tp_count) * share, share, 1)
        for d in range(-3, 5)
    }
    outs = []
    for first_row, rows in RINGS:
        attended = attend(first_row, rows, own_codes, q, k, v, arrays, from_partner)

        def part(offset, attended=attended):
            return jnp.dot(attended, weights[offset], preferred_element_type=jnp.float32)

        far = part(4).astype(jnp.bfloat16)
        up = lax.ppermute(far[:, :half], "tp", ring_up)
        dn = lax.ppermute(far[:, half:], "tp", ring_dn)
        zeros = jnp.zeros((rows, half), jnp.bfloat16)
        up = jnp.concatenate([up, zeros], axis=1)
        dn = jnp.concatenate([zeros, dn], axis=1)
        for d in (3, 2, 1):
            up = (part(d) + up.astype(jnp.float32)).astype(jnp.bfloat16)
            up = lax.ppermute(up, "tp", ring_up)
            dn = (part(-d) + dn.astype(jnp.float32)).astype(jnp.bfloat16)
            dn = lax.ppermute(dn, "tp", ring_dn)
        outs.append((part(0) + up.astype(jnp.float32) + dn.astype(jnp.float32)).astype(jnp.bfloat16))
    return jnp.concatenate(outs, axis=0)[None]


def solution(mesh):
    placed = (
        P(None, "ctx", "tp"),
        P(None, "ctx", "tp"),
        P(None, "ctx", "tp"),
        P(None, "ctx", "tp", None),
        P("tp", None),
    )
    return jax.shard_map(
        layer, mesh=mesh, in_specs=placed, out_specs=P(None, "ctx", "tp"), check_vma=False
    )
```
